32 devices in a mesh: walk: 8 (over y, x, core), tan: 4 (over z).
Axes of the slice: x: 2, y: 2, z: 4, core: 2. Of those that a mesh axis runs over, the one named last changes fastest.
Arguments:
- primal: float32 [32, 64, 256], P('walk'), may hold values from -6 to 6
- laplace: float32 [32, 64, 256], P('walk'), may hold values from -6 to 6
- tangent: bfloat16 [192, 32, 64, 256], P('tan', 'walk'), may hold values from -0.59765625 to 0.59765625
- cot_primal: float32 [32, 64, 256], P('walk'), may hold values from -6 to 6
- cot_tangent: bfloat16 [192, 32, 64, 256], P('tan', 'walk'), may hold values from -0.59765625 to 0.59765625
- cot_laplace: float32 [32, 64, 256], P('walk'), may hold values from -1.8 to 1.8
- weight: bfloat16 [256, 256], replicated, may hold values from -0.375 to 0.375
- bias: float32 [256], replicated, may hold values from -3 to 3
Outputs:
- grad_primal: float32 [32, 64, 256], P('walk')
- grad_laplace: float32 [32, 64, 256], P('walk')
- grad_tangent: bfloat16 [192, 32, 64, 256], P('tan', 'walk')
- grad_weight: float32 [256, 256], replicated
- grad_bias: float32 [256], replicated
The draws below stay inside these ranges and needn't reach their ends.
All inputs are finite; a program needn't handle non-finite values.
Results may differ from the reference program's by a relative error of at most 0.0034.
Values sent between devices are 32-bit elements; how exact they have to be, the bound alone decides.
A program may use at most 64 MiB of HBM per device.

```python
import jax
import jax.numpy as jnp
from jax import lax

D = 256
ELEC = 64
CHANNELS = 192
WALKERS = 32


def steps_of(rng, shape, split, least, high):
    def one(dim, shards_of):
        steps = jax.random.uniform(jax.random.fold_in(jax.random.fold_in(rng, 6), dim), (shards_of,), jnp.float32, least / len(split), high / len(split))
        return jnp.repeat(jnp.exp(steps), shape[dim] // shards_of).reshape((-1,) + (1,) * (len(shape) - dim - 1))

    factor_of = one(*split[0])
    for cut in split[1:]:
        factor_of = factor_of * one(*cut)
    return factor_of


def normal_values(stream_key, shape, scale, limit, pieces=(), dtype=jnp.bfloat16):
    loudness = steps_of(stream_key, shape, pieces, -0.22, 0.18) if pieces else 1.0
    drawn = jax.random.normal(stream_key, shape, jnp.float32) * scale * loudness
    return jnp.minimum(jnp.maximum(drawn, -limit), limit).astype(dtype)


def setup_inputs(seed: int = 0) -> dict:
    seeds = jax.random.split(jax.random.key(seed), 9)
    primal = normal_values(seeds[0], (WALKERS, ELEC, D), 1.0, 6.0, ((0, 8),), jnp.float32)
    laplace = normal_values(seeds[1], (WALKERS, ELEC, D), 1.0, 6.0, ((0, 8),), jnp.float32)
    tangent = normal_values(seeds[2], (CHANNELS, WALKERS, ELEC, D), 0.1, 0.59765625, ((0, 4), (1, 8)))
    cot_primal = normal_values(seeds[3], (WALKERS, ELEC, D), 1.0, 6.0, ((0, 8),), jnp.float32)
    cot_tangent = normal_values(seeds[4], (CHANNELS, WALKERS, ELEC, D), 0.1, 0.59765625, ((0, 4), (1, 8)))
    cot_laplace = normal_values(seeds[5], (WALKERS, ELEC, D), 0.3, 1.8, ((0, 8),), jnp.float32)
    weight = normal_values(seeds[6], (D, D), D ** -0.5, 0.375)
    bias = normal_values(seeds[7], (D,), 0.5, 3.0, (), jnp.float32)
    return {"primal": primal, "laplace": laplace, "tangent": tangent, "cot_primal": cot_primal, "cot_tangent": cot_tangent, "cot_laplace": cot_laplace, "weight": weight, "bias": bias}


def reference(primal, laplace, tangent, cot_primal, cot_tangent, cot_laplace, weight, bias):
    high = lax.Precision.HIGHEST
    weight_wide = weight.astype(jnp.float32)
    rows = primal.reshape(-1, D)
    lap_rows = laplace.reshape(-1, D)
    pre = jnp.dot(rows, weight_wide, precision=high) + bias
    tanh_pre = jnp.tanh(pre)
    slope = 1.0 - tanh_pre * tanh_pre
    curve = -2.0 * tanh_pre * slope
    third = (6.0 * tanh_pre * tanh_pre - 2.0) * slope
    lap_pre = jnp.dot(lap_rows, weight_wide, precision=high)
    tan_flat = tangent.reshape(CHANNELS, -1, D)
    cot_flat = cot_tangent.reshape(CHANNELS, -1, D)

    def accumulate(carry, pair):
        tan_one, cot_one = pair
        moved = jnp.dot(tan_one, weight, preferred_element_type=jnp.float32)
        return (carry[0] + moved * moved, carry[1] + cot_one.astype(jnp.float32) * moved), None

    zeros = jnp.zeros(rows.shape, jnp.float32)
    (squares, crossed), _ = lax.scan(accumulate, (zeros, zeros), (tan_flat, cot_flat))
    cot_rows = cot_primal.reshape(-1, D)
    cot_lap = cot_laplace.reshape(-1, D)
    grad_pre = cot_rows * slope + cot_lap * (curve * lap_pre + third * squares) + curve * crossed
    grad_lap_pre = cot_lap * slope

    def backward(total, pair):
        tan_one, cot_one = pair
        moved = jnp.dot(tan_one, weight, preferred_element_type=jnp.float32)
        grad_moved = (slope * cot_one.astype(jnp.float32) + 2.0 * curve * cot_lap * moved).astype(jnp.bfloat16)
        result = (cot_one.astype(jnp.float32) + jnp.dot(grad_moved, weight.T, preferred_element_type=jnp.float32)).astype(jnp.bfloat16)
        total = total + lax.dot_general(tan_one, grad_moved, (((0,), (0,)), ((), ())), preferred_element_type=jnp.float32)
        return total, result

    tangent_term, grad_tan = lax.scan(backward, jnp.zeros((D, D), jnp.float32), (tan_flat, cot_flat))
    grad_primal = cot_rows + jnp.dot(grad_pre, weight_wide.T, precision=high)
    grad_laplace = cot_lap + jnp.dot(grad_lap_pre, weight_wide.T, precision=high)
    dims = (((0,), (0,)), ((), ()))
    grad_weight = tangent_term + lax.dot_general(rows, grad_pre, dims, precision=high) + lax.dot_general(lap_rows, grad_lap_pre, dims, precision=high)
    grad_bias = jnp.sum(grad_pre, 0)
    return (grad_primal.reshape(primal.shape), grad_laplace.reshape(primal.shape), grad_tan.reshape(tangent.shape), grad_weight, grad_bias)
```

```python
import functools

import jax
import jax.numpy as jnp
from jax import lax
from jax.experimental import pallas as pl
from jax.experimental.pallas import tpu as pltpu
from jax.sharding import PartitionSpec as P

F32 = jnp.float32
BF16 = jnp.bfloat16
MESH = pl.DeviceIdType.MESH
TRANS_B = (((1,), (1,)), ((), ()))
TRANS_A = (((0,), (0,)), ((), ()))
PLAIN = (((1,), (0,)), ((), ()))


def mm(a, b, dims=PLAIN):
    return lax.dot_general(a, b, dims, preferred_element_type=F32)


def halves(x):
    top = x.astype(BF16)
    return top, (x - top.astype(F32)).astype(BF16)


def wide_mm(x, w, dims):
    top, low = halves(x)
    return mm(top, w, dims) + mm(low, w, dims)


def wide_outer(x, y):
    xt, xl = halves(x)
    yt, yl = halves(y)
    return mm(xt, yt, TRANS_A) + mm(xt, yl, TRANS_A) + mm(xl, yt, TRANS_A)


def local_kernel(
    group, shares, primal, laplace, tangent, cot_primal, cot_tangent, cot_laplace, weight, bias,
    grad_lap, grad_tan, share, grad_w, grad_b, moved_back,
):
    channels, rows, width = tangent.shape
    w = weight[...]
    pre = wide_mm(primal[...], w, PLAIN) + bias[...]
    t = jnp.tanh(pre)
    s1 = 1.0 - t * t
    s2 = -2.0 * t * s1
    s3 = (6.0 * t * t - 2.0) * s1
    lz = wide_mm(laplace[...], w, PLAIN)
    cl = cot_laplace[...]
    g_lz = cl * s1
    grad_lap[...] = cl + wide_mm(g_lz, w, TRANS_B)
    a = 2.0 * s2 * cl

    def step(i, carry):
        q, r = carry
        at = pl.ds(i * group, group)
        tan = tangent[at].reshape(group * rows, width)
        cot = cot_tangent[at].astype(F32)
        dz = mm(tan, w).reshape(group, rows, width)
        q = q + jnp.sum(dz * dz, 0)
        r = r + jnp.sum(cot * dz, 0)
        g = (s1[None] * cot + a[None] * dz).astype(BF16).reshape(group * rows, width)
        moved_back[pl.ds(i * group * rows, group * rows), :] = g
        back = mm(g, w, TRANS_B).reshape(group, rows, width)
        grad_tan[at] = (cot + back).astype(BF16)
        return q, r

    zero = jnp.zeros((rows, width), F32)
    q, r = lax.fori_loop(0, channels // group, step, (zero, zero), unroll=True)
    v = (cl * s3 * q + s2 * r) + (cot_primal[...] * s1 + cl * (s2 * lz)) * (1.0 / shares)
    share[...] = v
    gw = mm(tangent[...].reshape(channels * rows, width), moved_back[...], TRANS_A)
    gw = gw + wide_outer(primal[...], v) + wide_outer(laplace[...], g_lz * (1.0 / shares))
    gb = jnp.broadcast_to(jnp.sum(v, 0, keepdims=True), grad_b.shape)

    @pl.when(pl.program_id(0) == 0)
    def _():
        grad_w[...] = gw
        grad_b[...] = gb

    @pl.when(pl.program_id(0) > 0)
    def _():
        grad_w[...] += gw
        grad_b[...] += gb


def sum_kernel(
    walks, tans, chunks, share, part_w, part_b, cot_primal, weight,
    grad_primal, grad_w, grad_b,
    x, r1, a1, r2, a2, r3, y, inner, outer, fin,
    s_core, r_core, s_chip, r_chip, s_tan, r_tan, s_back, r_back, s_last, r_last,
    s_in, r_in, r_fin, s_out,
):
    teams = walks // 2
    walk, tan = lax.axis_index("walk"), lax.axis_index("tan")
    core, team = lax.rem(walk, 2), walk // 2
    mate = team * 2 + (1 - core)
    width = share.shape[1]
    piece = part_w.shape[0] // walks
    size = share.shape[0] // chunks

    def to(w, t):
        return (w, t)

    mates = [to(mate, tan)]
    crew = [to(lax.rem(team + d, teams) * 2 + core, tan) for d in range(1, teams)]
    line = [to(walk, lax.rem(tan + d, tans)) for d in range(1, tans)]

    barrier = pltpu.get_barrier_semaphore()
    for who in mates + crew + line:
        pl.semaphore_signal(barrier, inc=1, device_id=who, device_id_type=MESH)

    for c in range(2):
        for k in range(teams):
            at = (k * 2 + c) * piece
            x[c, k, 0:piece, :] = part_w[at : at + piece, :]
            x[c, k, piece:, :] = part_b[...]
    pl.semaphore_wait(barrier, 1 + (teams - 1) + (tans - 1))

    def copy(src, dst, s, r, who):
        return pltpu.make_async_remote_copy(
            src_ref=src, dst_ref=dst, send_sem=s, recv_sem=r, device_id=who, device_id_type=MESH
        )

    first = copy(x.at[1 - core], r1, s_core, r_core, mates[0])
    first.start()

    half = tans // 2
    left = tan < half
    pos = jnp.where(left, tan, tans - 1 - tan)
    inward = to(walk, jnp.where(left, tan + 1, tan - 1))
    outward = to(walk, jnp.where(left, jnp.maximum(tan - 1, 0), jnp.minimum(tan + 1, tans - 1)))
    end, middle = pos == 0, pos == half - 1

    def rows_of(k):
        return pl.ds(k * size, size)

    def in_copy(src, k):
        return copy(src, inner.at[k], s_in.at[k], r_in.at[k], inward)

    def cross_copy(src, k):
        return copy(src, fin.at[k], s_in.at[k], r_fin.at[k], inward)

    def out_copy(src, k):
        return copy(src, fin.at[k], s_out.at[k], r_fin.at[k], outward)

    def send_in(src, k):
        @pl.when(middle)
        def _():
            cross_copy(src, k).start()

        @pl.when(jnp.logical_not(middle))
        def _():
            in_copy(src, k).start()

    @pl.when(end)
    def _():
        for k in range(chunks):
            send_in(share.at[rows_of(k)], k)

    first.wait()
    a1[...] = x[core] + r1[...]
    seconds = []
    for d in range(1, teams):
        c = copy(a1.at[lax.rem(team + d, teams)], r2.at[d - 1], s_chip.at[d - 1], r_chip.at[d - 1], crew[d - 1])
        c.start()
        seconds.append(c)

    @pl.when(jnp.logical_not(end))
    def _():
        for k in range(chunks):
            in_copy(share.at[rows_of(k)], k).wait_recv()
            outer[k] = share[rows_of(k), :] + inner[k]
            send_in(outer.at[k], k)

    for c in seconds:
        c.wait()
    total = a1[team]
    for d in range(teams - 1):
        total = total + r2[d]
    a2[...] = total
    thirds = []
    for d in range(1, tans):
        c = copy(a2, r3.at[tan], s_tan.at[d - 1], r_tan.at[d - 1], line[d - 1])
        c.start()
        thirds.append(c)
    r3[tan] = total

    w = weight[...]

    def finish(k):
        cross_copy(share.at[rows_of(k)], k).wait_recv()

        @pl.when(middle)
        def _():
            @pl.when(end)
            def _():
                fin[k] = share[rows_of(k), :] + fin[k]

            @pl.when(jnp.logical_not(end))
            def _():
                fin[k] = outer[k] + fin[k]

        @pl.when(jnp.logical_not(end))
        def _():
            out_copy(fin.at[k], k).start()

        grad_primal[rows_of(k), :] = cot_primal[rows_of(k), :] + wide_mm(fin[k], w, TRANS_B)

    for k in range(chunks):
        finish(k)

    for c in thirds:
        c.wait()
    total = r3[0]
    for t in range(1, tans):
        total = total + r3[t]
    y[core, team] = total
    fourths = []
    for d in range(1, teams):
        c = copy(y.at[core, team], y.at[core, team], s_back.at[d - 1], r_back.at[d - 1], crew[d - 1])
        c.start()
        fourths.append(c)
    for c in fourths:
        c.wait()
    last = copy(y.at[core], y.at[core], s_last, r_last, mates[0])
    last.start()
    last.wait()
    for c in range(2):
        for k in range(teams):
            at = (k * 2 + c) * piece
            grad_w[at : at + piece, :] = y[c, k, 0:piece, :]
    grad_b[...] = y[0, 0, piece : piece + 1, :]

    for k in range(chunks):
        cross_copy(share.at[rows_of(k)], k).wait_send()

        @pl.when(jnp.logical_not(end))
        def _():
            out_copy(fin.at[k], k).wait_send()


def per_device(walks, tans, primal, laplace, tangent, cot_primal, cot_tangent, cot_laplace, weight, bias):
    walkers, electrons, width = primal.shape
    channels = tangent.shape[0]
    rows = walkers * electrons
    flat = [z.reshape(rows, width) for z in (primal, laplace, cot_primal, cot_laplace)]
    tan_flat = tangent.reshape(channels, rows, width)
    cot_flat = cot_tangent.reshape(channels, rows, width)
    bias_row = bias.reshape(1, width)
    block = electrons
    group = next(g for g in (4, 3, 2, 1) if channels % g == 0)
    row_spec = pl.BlockSpec((block, width), lambda i: (i, 0))
    tan_spec = pl.BlockSpec((channels, block, width), lambda i: (0, i, 0))

    def whole(shape):
        return pl.BlockSpec(shape, lambda i: (0,) * len(shape))

    grad_lap, grad_tan, share, part_w, part_b = pl.pallas_call(
        functools.partial(local_kernel, group, tans),
        grid=(rows // block,),
        in_specs=[row_spec, row_spec, tan_spec, row_spec, tan_spec, row_spec, whole((width, width)), whole((1, width))],
        out_specs=[row_spec, tan_spec, row_spec, whole((width, width)), whole((8, width))],
        out_shape=[
            jax.ShapeDtypeStruct((rows, width), F32),
            jax.ShapeDtypeStruct(tan_flat.shape, BF16),
            jax.ShapeDtypeStruct((rows, width), F32),
            jax.ShapeDtypeStruct((width, width), F32),
            jax.ShapeDtypeStruct((8, width), F32),
        ],
        scratch_shapes=[pltpu.VMEM((channels * block, width), BF16)],
        compiler_params=pltpu.CompilerParams(vmem_limit_bytes=48 * 1024 * 1024),
        name="local",
    )(flat[0], flat[1], tan_flat, flat[2], cot_flat, flat[3], weight, bias_row)

    teams = walks // 2
    piece = width // walks + 8
    chunks = walkers
    size = rows // chunks
    vmem = pl.BlockSpec(memory_space=pltpu.VMEM)
    dma = pltpu.SemaphoreType.DMA
    crew, line = max(teams - 1, 1), max(tans - 1, 1)
    grad_primal, grad_w, grad_b = pl.pallas_call(
        functools.partial(sum_kernel, walks, tans, chunks),
        in_specs=[vmem] * 5,
        out_specs=[vmem] * 3,
        out_shape=[
            jax.ShapeDtypeStruct((rows, width), F32),
            jax.ShapeDtypeStruct((width, width), F32),
            jax.ShapeDtypeStruct((1, width), F32),
        ],
        scratch_shapes=[
            pltpu.VMEM((2, teams, piece, width), F32),
            pltpu.VMEM((teams, piece, width), F32),
            pltpu.VMEM((teams, piece, width), F32),
            pltpu.VMEM((crew, piece, width), F32),
            pltpu.VMEM((piece, width), F32),
            pltpu.VMEM((tans, piece, width), F32),
            pltpu.VMEM((2, teams, piece, width), F32),
            pltpu.VMEM((chunks, size, width), F32),
            pltpu.VMEM((chunks, size, width), F32),
            pltpu.VMEM((chunks, size, width), F32),
            dma, dma,
            dma((crew,)), dma((crew,)),
            dma((line,)), dma((line,)),
            dma((crew,)), dma((crew,)),
            dma, dma,
            dma((chunks,)), dma((chunks,)), dma((chunks,)), dma((chunks,)),
        ],
        compiler_params=pltpu.CompilerParams(collective_id=0, has_side_effects=True),
        name="sums",
    )(share, part_w, part_b, flat[2], weight)
    return (
        grad_primal.reshape(primal.shape),
        grad_lap.reshape(primal.shape),
        grad_tan.reshape(tangent.shape),
        grad_w,
        grad_b.reshape(bias.shape),
    )


def solution(mesh):
    return jax.shard_map(
        functools.partial(per_device, mesh.shape["walk"], mesh.shape["tan"]),
        mesh=mesh,
        in_specs=(
            P("walk", None, None),
            P("walk", None, None),
            P("tan", "walk", None, None),
            P("walk", None, None),
            P("tan", "walk", None, None),
            P("walk", None, None),
            P(),
            P(),
        ),
        out_specs=(
            P("walk", None, None),
            P("walk", None, None),
            P("tan", "walk", None, None),
            P(),
            P(),
        ),
        check_vma=False,
    )
```

```python
import functools

import jax
import jax.numpy as jnp
from jax import lax
from jax.experimental import pallas as pl
from jax.experimental.pallas import tpu as pltpu
from jax.sharding import PartitionSpec as P

F32 = jnp.float32
BF16 = jnp.bfloat16
MESH = pl.DeviceIdType.MESH
VMEM_ALL = 67_043_328
TRANS_B = (((1,), (1,)), ((), ()))
TRANS_A = (((0,), (0,)), ((), ()))
PLAIN = (((1,), (0,)), ((), ()))


def mm(a, b, dims=PLAIN):
    return lax.dot_general(a, b, dims, preferred_element_type=F32)


def halves(x):
    top = x.astype(BF16)
    return top, (x - top.astype(F32)).astype(BF16)


def wide_mm(x, w, dims):
    top, low = halves(x)
    return mm(top, w, dims) + mm(low, w, dims)


def wide_outer(x, y):
    xt, xl = halves(x)
    yt, yl = halves(y)
    return mm(xt, yt, TRANS_A) + mm(xt, yl, TRANS_A) + mm(xl, yt, TRANS_A)


def local_kernel(
    group, span, shares, primal, laplace, tangent, cot_primal, cot_tangent, cot_laplace, weight, bias,
    grad_lap, grad_tan, share, grad_w, grad_b, moved, moved_back, slope, gain, squares, crossed,
):
    channels, rows, width = tangent.shape
    w = weight[...]
    pre = wide_mm(primal[...], w, PLAIN) + bias[...]
    t = jnp.tanh(pre)
    s1 = 1.0 - t * t
    s2 = -2.0 * t * s1
    s3 = (6.0 * t * t - 2.0) * s1
    lz = wide_mm(laplace[...], w, PLAIN)
    cl = cot_laplace[...]
    g_lz = cl * s1
    grad_lap[...] = cl + wide_mm(g_lz, w, TRANS_B)
    slope[...] = s1
    gain[...] = 2.0 * s2 * cl
    tile = 16
    flat_rows = group * rows
    count = channels // group

    def forward(j):
        at = pl.ds(j * group, group)
        moved[at] = mm(tangent[at].reshape(flat_rows, width), w).reshape(group, rows, width)

    def middle(j):
        for k in range(0, rows, tile):
            row = pl.ds(k, tile)
            s, a = slope[row, :], gain[row, :]
            if j == 0:
                q = jnp.zeros((tile, width), F32)
                r = jnp.zeros((tile, width), F32)
            else:
                q, r = squares[row, :], crossed[row, :]
            for c in range(j * group, (j + 1) * group):
                dz = moved[c, row, :]
                cot = cot_tangent[c, row, :].astype(F32)
                q = q + dz * dz
                r = r + cot * dz
                moved_back[c, row, :] = (s * cot + a * dz).astype(BF16)
            squares[row, :], crossed[row, :] = q, r

    def backward(j):
        at = pl.ds(j * group, group)
        g = moved_back[at].reshape(flat_rows, width)
        back = mm(g, w, TRANS_B).reshape(group, rows, width)
        grad_tan[at] = (cot_tangent[at].astype(F32) + back).astype(BF16)

    @pl.when(pl.program_id(0) == 0)
    def _():
        grad_w[...] = jnp.zeros_like(grad_w)
        grad_b[...] = jnp.zeros_like(grad_b)

    forward(0)
    for j in range(count):
        if j + 1 < count:
            forward(j + 1)
        middle(j)
        backward(j)
        if (j + 1) % span == 0:
            at = pl.ds((j + 1 - span) * group, span * group)
            deep = span * flat_rows
            grad_w[...] += mm(tangent[at].reshape(deep, width), moved_back[at].reshape(deep, width), TRANS_A)
    v = (cl * s3 * squares[...] + s2 * crossed[...]) + (cot_primal[...] * s1 + cl * (s2 * lz)) * (1.0 / shares)
    share[...] = v
    grad_w[...] += wide_outer(primal[...], v) + wide_outer(laplace[...], g_lz * (1.0 / shares))
    grad_b[...] += jnp.broadcast_to(jnp.sum(v, 0, keepdims=True), grad_b.shape)


def sum_kernel(
    walks, tans, chunks, share, part_w, part_b,
    pre_out, y_out,
    x, r1, a1, r2, a2, inner, outer, fin, inner_w, outer_w, fin_w, y,
    s_core, r_core, s_chip, r_chip, s_back, r_back, s_last, r_last,
    s_in, r_in, r_fin, s_out,
):
    teams = walks // 2
    walk, tan = lax.axis_index("walk"), lax.axis_index("tan")
    core, team = lax.rem(walk, 2), walk // 2
    mate = team * 2 + (1 - core)
    width = share.shape[1]
    piece = part_w.shape[0] // walks
    size = share.shape[0] // chunks

    def to(w, t):
        return (w, t)

    mates = [to(mate, tan)]
    crew = [to(lax.rem(team + d, teams) * 2 + core, tan) for d in range(1, teams)]
    line = [to(walk, lax.rem(tan + d, tans)) for d in range(1, tans)]

    barrier = pltpu.get_barrier_semaphore()
    for who in mates + crew + line:
        pl.semaphore_signal(barrier, inc=1, device_id=who, device_id_type=MESH)

    for c in range(2):
        for k in range(teams):
            at = (k * 2 + c) * piece
            x[c, k, 0:piece, :] = part_w[at : at + piece, :]
            x[c, k, piece:, :] = part_b[...]
    pl.semaphore_wait(barrier, 1 + (teams - 1) + (tans - 1))

    def copy(src, dst, s, r, who):
        return pltpu.make_async_remote_copy(
            src_ref=src, dst_ref=dst, send_sem=s, recv_sem=r, device_id=who, device_id_type=MESH
        )

    first = copy(x.at[1 - core], r1, s_core, r_core, mates[0])
    first.start()

    half = tans // 2
    left = tan < half
    pos = jnp.where(left, tan, tans - 1 - tan)
    inward = to(walk, jnp.where(left, tan + 1, tan - 1))
    outward = to(walk, jnp.where(left, jnp.maximum(tan - 1, 0), jnp.minimum(tan + 1, tans - 1)))
    end, middle = pos == 0, pos == half - 1

    def mine(k):
        return a2 if k == chunks else share.at[pl.ds(k * size, size)]

    def inner_of(k):
        return inner_w if k == chunks else inner.at[k]

    def outer_of(k):
        return outer_w if k == chunks else outer.at[k]

    def fin_of(k):
        return fin_w if k == chunks else fin.at[k]

    def in_copy(src, k):
        return copy(src, inner_of(k), s_in.at[k], r_in.at[k], inward)

    def cross_copy(src, k):
        return copy(src, fin_of(k), s_in.at[k], r_fin.at[k], inward)

    def out_copy(k):
        return copy(fin_of(k), fin_of(k), s_out.at[k], r_fin.at[k], outward)

    def send_in(src, k):
        @pl.when(middle)
        def _():
            cross_copy(src, k).start()

        @pl.when(jnp.logical_not(middle))
        def _():
            in_copy(src, k).start()

    def begin(k):
        @pl.when(end)
        def _():
            send_in(mine(k), k)

    def relay(k):
        @pl.when(jnp.logical_not(end))
        def _():
            in_copy(mine(k), k).wait_recv()
            outer_of(k)[...] = mine(k)[...] + inner_of(k)[...]
            send_in(outer_of(k), k)

    def finish(k):
        cross_copy(mine(k), k).wait_recv()
        f = fin_of(k)

        @pl.when(jnp.logical_and(middle, end))
        def _():
            f[...] = mine(k)[...] + f[...]

        @pl.when(jnp.logical_and(middle, jnp.logical_not(end)))
        def _():
            f[...] = outer_of(k)[...] + f[...]

        @pl.when(jnp.logical_not(end))
        def _():
            out_copy(k).start()

    for k in range(chunks):
        begin(k)

    first.wait()
    a1[...] = x[core] + r1[...]
    seconds = []
    for d in range(1, teams):
        c = copy(a1.at[lax.rem(team + d, teams)], r2.at[d - 1], s_chip.at[d - 1], r_chip.at[d - 1], crew[d - 1])
        c.start()
        seconds.append(c)

    for k in range(chunks):
        relay(k)

    for c in seconds:
        c.wait()
    total = a1[team]
    for d in range(teams - 1):
        total = total + r2[d]
    a2[...] = total
    begin(chunks)
    for k in range(chunks):
        if k == chunks // 2:
            relay(chunks)
        finish(k)
        pre_out[pl.ds(k * size, size), :] = fin[k]
    finish(chunks)

    y[core, team] = fin_w[...]
    fourths = []
    for d in range(1, teams):
        c = copy(y.at[core, team], y.at[core, team], s_back.at[d - 1], r_back.at[d - 1], crew[d - 1])
        c.start()
        fourths.append(c)
    for c in fourths:
        c.wait()
    last = copy(y.at[core], y.at[core], s_last, r_last, mates[0])
    last.start()
    last.wait()
    y_out[...] = y[...]

    for k in range(chunks + 1):
        cross_copy(mine(k), k).wait_send()

        @pl.when(jnp.logical_not(end))
        def _():
            out_copy(k).wait_send()


def finish_kernel(walks, pre, y, cot_primal, weight, grad_primal, grad_w, grad_b):
    piece = grad_w.shape[0] // walks
    grad_primal[...] = cot_primal[...] + wide_mm(pre[...], weight[...], TRANS_B)
    for c in range(2):
        for k in range(walks // 2):
            at = (k * 2 + c) * piece
            grad_w[at : at + piece, :] = y[c, k, 0:piece, :]
    grad_b[...] = y[0, 0, piece : piece + 1, :]


def per_device(walks, tans, primal, laplace, tangent, cot_primal, cot_tangent, cot_laplace, weight, bias):
    walkers, electrons, width = primal.shape
    channels = tangent.shape[0]
    rows = walkers * electrons
    flat = [z.reshape(rows, width) for z in (primal, laplace, cot_primal, cot_laplace)]
    tan_flat = tangent.reshape(channels, rows, width)
    cot_flat = cot_tangent.reshape(channels, rows, width)
    bias_row = bias.reshape(1, width)
    block = electrons
    group = next(g for g in (8, 6, 4, 3, 2, 1) if channels % g == 0)
    span = next(g for g in (2, 3, 1) if channels // group % g == 0)
    row_spec = pl.BlockSpec((block, width), lambda i: (i, 0))
    tan_spec = pl.BlockSpec((channels, block, width), lambda i: (0, i, 0))

    def whole(shape):
        return pl.BlockSpec(shape, lambda i: (0,) * len(shape))

    grad_lap, grad_tan, share, part_w, part_b = pl.pallas_call(
        functools.partial(local_kernel, group, span, tans),
        grid=(rows // block,),
        in_specs=[row_spec, row_spec, tan_spec, row_spec, tan_spec, row_spec, whole((width, width)), whole((1, width))],
        out_specs=[row_spec, tan_spec, row_spec, whole((width, width)), whole((8, width))],
        out_shape=[
            jax.ShapeDtypeStruct((rows, width), F32),
            jax.ShapeDtypeStruct(tan_flat.shape, BF16),
            jax.ShapeDtypeStruct((rows, width), F32),
            jax.ShapeDtypeStruct((width, width), F32),
            jax.ShapeDtypeStruct((8, width), F32),
        ],
        scratch_shapes=[pltpu.VMEM((channels, block, width), F32), pltpu.VMEM((channels, block, width), BF16)]
        + [pltpu.VMEM((block, width), F32)] * 4,
        compiler_params=pltpu.CompilerParams(vmem_limit_bytes=VMEM_ALL),
        name="local",
    )(flat[0], flat[1], tan_flat, flat[2], cot_flat, flat[3], weight, bias_row)

    teams = walks // 2
    piece = width // walks + 8
    chunks = walkers
    size = rows // chunks
    vmem = pl.BlockSpec(memory_space=pltpu.VMEM)
    dma = pltpu.SemaphoreType.DMA
    crew = max(teams - 1, 1)
    pre_sum, y = pl.pallas_call(
        functools.partial(sum_kernel, walks, tans, chunks),
        in_specs=[vmem] * 3,
        out_specs=[vmem] * 2,
        out_shape=[
            jax.ShapeDtypeStruct((rows, width), F32),
            jax.ShapeDtypeStruct((2, teams, piece, width), F32),
        ],
        scratch_shapes=[
            pltpu.VMEM((2, teams, piece, width), F32),
            pltpu.VMEM((teams, piece, width), F32),
            pltpu.VMEM((teams, piece, width), F32),
            pltpu.VMEM((crew, piece, width), F32),
            pltpu.VMEM((piece, width), F32),
            pltpu.VMEM((chunks, size, width), F32),
            pltpu.VMEM((chunks, size, width), F32),
            pltpu.VMEM((chunks, size, width), F32),
            pltpu.VMEM((piece, width), F32),
            pltpu.VMEM((piece, width), F32),
            pltpu.VMEM((piece, width), F32),
            pltpu.VMEM((2, teams, piece, width), F32),
            dma, dma,
            dma((crew,)), dma((crew,)),
            dma((crew,)), dma((crew,)),
            dma, dma,
            dma((chunks + 1,)), dma((chunks + 1,)), dma((chunks + 1,)), dma((chunks + 1,)),
        ],
        compiler_params=pltpu.CompilerParams(collective_id=0, has_side_effects=True, vmem_limit_bytes=VMEM_ALL),
        name="sums",
    )(share, part_w, part_b)
    grad_primal, grad_w, grad_b = pl.pallas_call(
        functools.partial(finish_kernel, walks),
        in_specs=[vmem] * 4,
        out_specs=[vmem] * 3,
        out_shape=[
            jax.ShapeDtypeStruct((rows, width), F32),
            jax.ShapeDtypeStruct((width, width), F32),
            jax.ShapeDtypeStruct((1, width), F32),
        ],
        compiler_params=pltpu.CompilerParams(vmem_limit_bytes=VMEM_ALL),
        name="finish",
    )(pre_sum, y, flat[2], weight)
    return (
        grad_primal.reshape(primal.shape),
        grad_lap.reshape(primal.shape),
        grad_tan.reshape(tangent.shape),
        grad_w,
        grad_b.reshape(bias.shape),
    )


def solution(mesh):
    return jax.shard_map(
        functools.partial(per_device, mesh.shape["walk"], mesh.shape["tan"]),
        mesh=mesh,
        in_specs=(
            P("walk", None, None),
            P("walk", None, None),
            P("tan", "walk", None, None),
            P("walk", None, None),
            P("tan", "walk", None, None),
            P("walk", None, None),
            P(),
            P(),
        ),
        out_specs=(
            P("walk", None, None),
            P("walk", None, None),
            P("tan", "walk", None, None),
            P(),
            P(),
        ),
        check_vma=False,
    )
```

```python
import functools

import jax
import jax.numpy as jnp
from jax import lax
from jax.experimental import pallas as pl
from jax.experimental.pallas import tpu as pltpu
from jax.sharding import PartitionSpec as P

F32 = jnp.float32
BF16 = jnp.bfloat16
MESH = pl.DeviceIdType.MESH
VMEM_ALL = 67_043_328
TRANS_B = (((1,), (1,)), ((), ()))
TRANS_A = (((0,), (0,)), ((), ()))
PLAIN = (((1,), (0,)), ((), ()))


def mm(a, b, dims=PLAIN):
    return lax.dot_general(a, b, dims, preferred_element_type=F32)


def halves(x):
    top = x.astype(BF16)
    return top, (x - top.astype(F32)).astype(BF16)


def wide_mm(x, w, dims):
    top, low = halves(x)
    return mm(top, w, dims) + mm(low, w, dims)


def wide_outer(x, y):
    xt, xl = halves(x)
    yt, yl = halves(y)
    return mm(xt, yt, TRANS_A) + mm(xt, yl, TRANS_A) + mm(xl, yt, TRANS_A)


def local_kernel(
    group, span, shares, primal, laplace, tangent, cot_primal, cot_tangent, cot_laplace, weight, bias,
    grad_lap, grad_tan, share, part, grad_w, grad_b, moved, moved_back, slope, gain, squares, crossed,
):
    channels, rows, width = tangent.shape
    w = weight[...]
    pre = wide_mm(primal[...], w, PLAIN) + bias[...]
    t = jnp.tanh(pre)
    s1 = 1.0 - t * t
    s2 = -2.0 * t * s1
    s3 = (6.0 * t * t - 2.0) * s1
    lz = wide_mm(laplace[...], w, PLAIN)
    cl = cot_laplace[...]
    g_lz = cl * s1
    grad_lap[...] = cl + wide_mm(g_lz, w, TRANS_B)
    slope[...] = s1
    gain[...] = 2.0 * s2 * cl
    tile = 16
    flat_rows = group * rows
    count = channels // group

    def forward(j):
        at = pl.ds(j * group, group)
        moved[at] = mm(tangent[at].reshape(flat_rows, width), w).reshape(group, rows, width)

    def middle(j):
        for k in range(0, rows, tile):
            row = pl.ds(k, tile)
            s, a = slope[row, :], gain[row, :]
            if j == 0:
                q = jnp.zeros((tile, width), F32)
                r = jnp.zeros((tile, width), F32)
            else:
                q, r = squares[row, :], crossed[row, :]
            for c in range(j * group, (j + 1) * group):
                dz = moved[c, row, :]
                cot = cot_tangent[c, row, :].astype(F32)
                q = q + dz * dz
                r = r + cot * dz
                moved_back[c, row, :] = (s * cot + a * dz).astype(BF16)
            squares[row, :], crossed[row, :] = q, r

    def backward(j):
        at = pl.ds(j * group, group)
        g = moved_back[at].reshape(flat_rows, width)
        back = mm(g, w, TRANS_B).reshape(group, rows, width)
        grad_tan[at] = (cot_tangent[at].astype(F32) + back).astype(BF16)

    @pl.when(pl.program_id(0) == 0)
    def _():
        grad_w[...] = jnp.zeros_like(grad_w)
        grad_b[...] = jnp.zeros_like(grad_b)

    forward(0)
    for j in range(count):
        if j + 1 < count:
            forward(j + 1)
        middle(j)
        if j > 0:
            backward(j - 1)
        if (j + 1) % span == 0:
            at = pl.ds((j + 1 - span) * group, span * group)
            deep = span * flat_rows
            grad_w[...] += mm(tangent[at].reshape(deep, width), moved_back[at].reshape(deep, width), TRANS_A)
    backward(count - 1)
    v = (cl * s3 * squares[...] + s2 * crossed[...]) + (cot_primal[...] * s1 + cl * (s2 * lz)) * (1.0 / shares)
    share[...] = v
    grad_w[...] += wide_outer(primal[...], v) + wide_outer(laplace[...], g_lz * (1.0 / shares))
    grad_b[...] += jnp.broadcast_to(jnp.sum(v, 0, keepdims=True), grad_b.shape)

    @pl.when(pl.program_id(0) == pl.num_programs(0) - 1)
    def _():
        piece = part.shape[2] - 8
        for c in range(2):
            for k in range(part.shape[1]):
                at = (k * 2 + c) * piece
                part[c, k, 0:piece, :] = grad_w[at : at + piece, :]
                part[c, k, piece:, :] = grad_b[...]


def sum_kernel(
    walks, tans, chunks, share_in, part,
    pre_out, y_out,
    share, x, r1, a1, r2, a2, inner, outer, fin, inner_w, outer_w, fin_w, y,
    s_core, r_core, s_chip, r_chip, s_back, r_back, s_last, r_last,
    s_in, r_in, r_fin, s_out, s_share, s_part,
):
    teams = walks // 2
    walk, tan = lax.axis_index("walk"), lax.axis_index("tan")
    core, team = lax.rem(walk, 2), walk // 2
    mate = team * 2 + (1 - core)
    size = share.shape[0] // chunks

    def to(w, t):
        return (w, t)

    mates = [to(mate, tan)]
    crew = [to(lax.rem(team + d, teams) * 2 + core, tan) for d in range(1, teams)]
    half = tans // 2
    left = tan < half
    pos = jnp.where(left, tan, tans - 1 - tan)
    inward = to(walk, jnp.where(left, tan + 1, tan - 1))
    outward = to(walk, jnp.where(left, jnp.maximum(tan - 1, 0), jnp.minimum(tan + 1, tans - 1)))
    end, middle = pos == 0, pos == half - 1

    barrier = pltpu.get_barrier_semaphore()
    greeted = mates + crew + [inward]
    for who in greeted:
        pl.semaphore_signal(barrier, inc=1, device_id=who, device_id_type=MESH)

    @pl.when(jnp.logical_not(end))
    def _():
        pl.semaphore_signal(barrier, inc=1, device_id=outward, device_id_type=MESH)

    load_part = pltpu.make_async_copy(part.at[core], x, s_part)
    load_part.start()
    load_share = pltpu.make_async_copy(share_in, share, s_share)
    load_share.start()

    @pl.when(end)
    def _():
        pl.semaphore_wait(barrier, len(greeted))

    @pl.when(jnp.logical_not(end))
    def _():
        pl.semaphore_wait(barrier, len(greeted) + 1)

    def copy(src, dst, s, r, who):
        return pltpu.make_async_remote_copy(
            src_ref=src, dst_ref=dst, send_sem=s, recv_sem=r, device_id=who, device_id_type=MESH
        )

    first = copy(part.at[1 - core], r1, s_core, r_core, mates[0])
    first.start()

    def mine(k):
        return a2 if k == chunks else share.at[pl.ds(k * size, size)]

    def inner_of(k):
        return inner_w if k == chunks else inner.at[k]

    def outer_of(k):
        return outer_w if k == chunks else outer.at[k]

    def fin_of(k):
        return fin_w if k == chunks else fin.at[k]

    def in_copy(src, k):
        return copy(src, inner_of(k), s_in.at[k], r_in.at[k], inward)

    def cross_copy(src, k):
        return copy(src, fin_of(k), s_in.at[k], r_fin.at[k], inward)

    def out_copy(k):
        return copy(fin_of(k), fin_of(k), s_out.at[k], r_fin.at[k], outward)

    def send_in(src, k):
        @pl.when(middle)
        def _():
            cross_copy(src, k).start()

        @pl.when(jnp.logical_not(middle))
        def _():
            in_copy(src, k).start()

    def begin(k):
        @pl.when(end)
        def _():
            send_in(a2 if k == chunks else share_in.at[pl.ds(k * size, size)], k)

    def relay(k):
        @pl.when(jnp.logical_not(end))
        def _():
            in_copy(mine(k), k).wait_recv()
            outer_of(k)[...] = mine(k)[...] + inner_of(k)[...]
            send_in(outer_of(k), k)

    def finish(k):
        cross_copy(mine(k), k).wait_recv()
        f = fin_of(k)

        @pl.when(jnp.logical_and(middle, end))
        def _():
            f[...] = mine(k)[...] + f[...]

        @pl.when(jnp.logical_and(middle, jnp.logical_not(end)))
        def _():
            f[...] = outer_of(k)[...] + f[...]

        @pl.when(jnp.logical_not(end))
        def _():
            out_copy(k).start()

    for k in range(chunks):
        begin(k)

    load_part.wait()
    load_share.wait()
    first.wait()
    a1[...] = x[...] + r1[...]
    seconds = []
    for d in range(1, teams):
        c = copy(a1.at[lax.rem(team + d, teams)], r2.at[d - 1], s_chip.at[d - 1], r_chip.at[d - 1], crew[d - 1])
        c.start()
        seconds.append(c)

    for k in range(chunks):
        relay(k)

    for c in seconds:
        c.wait()
    total = a1[team]
    for d in range(teams - 1):
        total = total + r2[d]
    a2[...] = total
    begin(chunks)
    for k in range(chunks):
        if k == chunks // 2:
            relay(chunks)
        finish(k)
        pre_out[pl.ds(k * size, size), :] = fin[k]
    finish(chunks)

    y[core, team] = fin_w[...]
    fourths = []
    for d in range(1, teams):
        c = copy(y.at[core, team], y.at[core, team], s_back.at[d - 1], r_back.at[d - 1], crew[d - 1])
        c.start()
        fourths.append(c)
    for c in fourths:
        c.wait()
    last = copy(y.at[core], y.at[core], s_last, r_last, mates[0])
    last.start()
    last.wait()
    y_out[...] = y[...]

    for k in range(chunks + 1):
        cross_copy(mine(k), k).wait_send()

        @pl.when(jnp.logical_not(end))
        def _():
            out_copy(k).wait_send()


def finish_kernel(walks, pre, y, cot_primal, weight, grad_primal, grad_w, grad_b):
    piece = grad_w.shape[0] // walks
    grad_primal[...] = cot_primal[...] + wide_mm(pre[...], weight[...], TRANS_B)
    for c in range(2):
        for k in range(walks // 2):
            at = (k * 2 + c) * piece
            grad_w[at : at + piece, :] = y[c, k, 0:piece, :]
    grad_b[...] = y[0, 0, piece : piece + 1, :]


def per_device(walks, tans, primal, laplace, tangent, cot_primal, cot_tangent, cot_laplace, weight, bias):
    walkers, electrons, width = primal.shape
    channels = tangent.shape[0]
    rows = walkers * electrons
    flat = [z.reshape(rows, width) for z in (primal, laplace, cot_primal, cot_laplace)]
    tan_flat = tangent.reshape(channels, rows, width)
    cot_flat = cot_tangent.reshape(channels, rows, width)
    bias_row = bias.reshape(1, width)
    block = electrons
    group = next(g for g in (8, 6, 4, 3, 2, 1) if channels % g == 0)
    span = next(g for g in (2, 3, 1) if channels // group % g == 0)
    row_spec = pl.BlockSpec((block, width), lambda i: (i, 0))
    tan_spec = pl.BlockSpec((channels, block, width), lambda i: (0, i, 0))

    def whole(shape):
        return pl.BlockSpec(shape, lambda i: (0,) * len(shape))

    teams = walks // 2
    piece = width // walks + 8
    grad_lap, grad_tan, share, part = pl.pallas_call(
        functools.partial(local_kernel, group, span, tans),
        grid=(rows // block,),
        in_specs=[row_spec, row_spec, tan_spec, row_spec, tan_spec, row_spec, whole((width, width)), whole((1, width))],
        out_specs=[row_spec, tan_spec, row_spec, whole((2, teams, piece, width))],
        out_shape=[
            jax.ShapeDtypeStruct((rows, width), F32),
            jax.ShapeDtypeStruct(tan_flat.shape, BF16),
            jax.ShapeDtypeStruct((rows, width), F32),
            jax.ShapeDtypeStruct((2, teams, piece, width), F32),
        ],
        scratch_shapes=[pltpu.VMEM((width, width), F32), pltpu.VMEM((8, width), F32)]
        + [pltpu.VMEM((channels, block, width), F32), pltpu.VMEM((channels, block, width), BF16)]
        + [pltpu.VMEM((block, width), F32)] * 4,
        compiler_params=pltpu.CompilerParams(vmem_limit_bytes=VMEM_ALL),
        name="local",
    )(flat[0], flat[1], tan_flat, flat[2], cot_flat, flat[3], weight, bias_row)

    chunks = walkers
    size = rows // chunks
    vmem = pl.BlockSpec(memory_space=pltpu.VMEM)
    dma = pltpu.SemaphoreType.DMA
    crew = max(teams - 1, 1)
    pre_sum, y = pl.pallas_call(
        functools.partial(sum_kernel, walks, tans, chunks),
        in_specs=[pl.BlockSpec(memory_space=pl.ANY)] * 2,
        out_specs=[vmem] * 2,
        out_shape=[
            jax.ShapeDtypeStruct((rows, width), F32),
            jax.ShapeDtypeStruct((2, teams, piece, width), F32),
        ],
        scratch_shapes=[
            pltpu.VMEM((rows, width), F32),
            pltpu.VMEM((teams, piece, width), F32),
            pltpu.VMEM((teams, piece, width), F32),
            pltpu.VMEM((teams, piece, width), F32),
            pltpu.VMEM((crew, piece, width), F32),
            pltpu.VMEM((piece, width), F32),
            pltpu.VMEM((chunks, size, width), F32),
            pltpu.VMEM((chunks, size, width), F32),
            pltpu.VMEM((chunks, size, width), F32),
            pltpu.VMEM((piece, width), F32),
            pltpu.VMEM((piece, width), F32),
            pltpu.VMEM((piece, width), F32),
            pltpu.VMEM((2, teams, piece, width), F32),
            dma, dma,
            dma((crew,)), dma((crew,)),
            dma((crew,)), dma((crew,)),
            dma, dma,
            dma((chunks + 1,)), dma((chunks + 1,)), dma((chunks + 1,)), dma((chunks + 1,)),
            dma, dma,
        ],
        compiler_params=pltpu.CompilerParams(collective_id=0, has_side_effects=True, vmem_limit_bytes=VMEM_ALL),
        name="sums",
    )(share, part)
    grad_primal, grad_w, grad_b = pl.pallas_call(
        functools.partial(finish_kernel, walks),
        in_specs=[vmem] * 4,
        out_specs=[vmem] * 3,
        out_shape=[
            jax.ShapeDtypeStruct((rows, width), F32),
            jax.ShapeDtypeStruct((width, width), F32),
            jax.ShapeDtypeStruct((1, width), F32),
        ],
        compiler_params=pltpu.CompilerParams(vmem_limit_bytes=VMEM_ALL),
        name="finish",
    )(pre_sum, y, flat[2], weight)
    return (
        grad_primal.reshape(primal.shape),
        grad_lap.reshape(primal.shape),
        grad_tan.reshape(tangent.shape),
        grad_w,
        grad_b.reshape(bias.shape),
    )


def solution(mesh):
    return jax.shard_map(
        functools.partial(per_device, mesh.shape["walk"], mesh.shape["tan"]),
        mesh=mesh,
        in_specs=(
            P("walk", None, None),
            P("walk", None, None),
            P("tan", "walk", None, None),
            P("walk", None, None),
            P("tan", "walk", None, None),
            P("walk", None, None),
            P(),
            P(),
        ),
        out_specs=(
            P("walk", None, None),
            P("walk", None, None),
            P("tan", "walk", None, None),
            P(),
            P(),
        ),
        check_vma=False,
    )
```

```python
import functools

import jax
import jax.numpy as jnp
from jax import lax
from jax.experimental import pallas as pl
from jax.experimental.pallas import tpu as pltpu
from jax.sharding import PartitionSpec as P

F32 = jnp.float32
BF16 = jnp.bfloat16
MESH = pl.DeviceIdType.MESH
VMEM_ALL = 67_043_328
TRANS_B = (((1,), (1,)), ((), ()))
TRANS_A = (((0,), (0,)), ((), ()))
PLAIN = (((1,), (0,)), ((), ()))


def mm(a, b, dims=PLAIN):
    return lax.dot_general(a, b, dims, preferred_element_type=F32)


def halves(x):
    top = x.astype(BF16)
    return top, (x - top.astype(F32)).astype(BF16)


def wide_mm(x, w, dims):
    top, low = halves(x)
    return mm(top, w, dims) + mm(low, w, dims)


def wide_outer(x, y):
    xt, xl = halves(x)
    yt, yl = halves(y)
    return mm(xt, yt, TRANS_A) + mm(xt, yl, TRANS_A) + mm(xl, yt, TRANS_A)


def local_kernel(
    group, span, shares, primal, laplace, tangent, cot_primal, cot_tangent, cot_laplace, weight, bias,
    grad_lap, grad_tan, share, part, grad_w, grad_b, moved, moved_back, slope, gain, squares, crossed,
):
    channels, rows, width = tangent.shape
    w = weight[...]
    pre = wide_mm(primal[...], w, PLAIN) + bias[...]
    t = jnp.tanh(pre)
    s1 = 1.0 - t * t
    s2 = -2.0 * t * s1
    s3 = (6.0 * t * t - 2.0) * s1
    lz = wide_mm(laplace[...], w, PLAIN)
    cl = cot_laplace[...]
    g_lz = cl * s1
    grad_lap[...] = cl + wide_mm(g_lz, w, TRANS_B)
    slope[...] = s1
    gain[...] = 2.0 * s2 * cl
    tile = 16
    flat_rows = group * rows
    count = channels // group

    def forward(j):
        at = pl.ds(j * group, group)
        moved[at] = mm(tangent[at].reshape(flat_rows, width), w).reshape(group, rows, width)

    def middle(j):
        for k in range(0, rows, tile):
            row = pl.ds(k, tile)
            s, a = slope[row, :], gain[row, :]
            if j == 0:
                q = jnp.zeros((tile, width), F32)
                r = jnp.zeros((tile, width), F32)
            else:
                q, r = squares[row, :], crossed[row, :]
            for c in range(j * group, (j + 1) * group):
                dz = moved[c, row, :]
                cot = cot_tangent[c, row, :].astype(F32)
                q = q + dz * dz
                r = r + cot * dz
                moved_back[c, row, :] = (s * cot + a * dz).astype(BF16)
            squares[row, :], crossed[row, :] = q, r

    def backward(j):
        at = pl.ds(j * group, group)
        g = moved_back[at].reshape(flat_rows, width)
        back = mm(g, w, TRANS_B).reshape(group, rows, width)
        grad_tan[at] = (cot_tangent[at].astype(F32) + back).astype(BF16)

    @pl.when(pl.program_id(0) == 0)
    def _():
        grad_w[...] = jnp.zeros_like(grad_w)
        grad_b[...] = jnp.zeros_like(grad_b)

    forward(0)
    for j in range(count):
        if j + 1 < count:
            forward(j + 1)
        middle(j)
        if j > 0:
            backward(j - 1)
        if (j + 1) % span == 0:
            at = pl.ds((j + 1 - span) * group, span * group)
            deep = span * flat_rows
            grad_w[...] += mm(tangent[at].reshape(deep, width), moved_back[at].reshape(deep, width), TRANS_A)
    backward(count - 1)
    v = (cl * s3 * squares[...] + s2 * crossed[...]) + (cot_primal[...] * s1 + cl * (s2 * lz)) * (1.0 / shares)
    share[...] = v
    grad_w[...] += wide_outer(primal[...], v) + wide_outer(laplace[...], g_lz * (1.0 / shares))
    grad_b[...] += jnp.broadcast_to(jnp.sum(v, 0, keepdims=True), grad_b.shape)

    @pl.when(pl.program_id(0) == pl.num_programs(0) - 1)
    def _():
        piece = part.shape[2] - 8
        for c in range(2):
            for k in range(part.shape[1]):
                at = (k * 2 + c) * piece
                part[c, k, 0:piece, :] = grad_w[at : at + piece, :]
                part[c, k, piece:, :] = grad_b[...]


def sum_kernel(
    walks, tans, chunks, share_in, part,
    pre_out, y_out,
    share, x, r1, a1, r2, a2, inner, outer, fin, inner_w, outer_w, fin_w, y,
    s_core, r_core, s_chip, r_chip, s_back, r_back, s_last, r_last,
    s_in, r_in, r_fin, s_out, s_share, s_part,
):
    teams = walks // 2
    walk, tan = lax.axis_index("walk"), lax.axis_index("tan")
    core, team = lax.rem(walk, 2), walk // 2
    mate = team * 2 + (1 - core)
    size = share.shape[0] // chunks

    def to(w, t):
        return (w, t)

    mates = [to(mate, tan)]
    crew = [to(lax.rem(team + d, teams) * 2 + core, tan) for d in range(1, teams)]
    half = tans // 2
    left = tan < half
    pos = jnp.where(left, tan, tans - 1 - tan)
    inward = to(walk, jnp.where(left, tan + 1, tan - 1))
    outward = to(walk, jnp.where(left, jnp.maximum(tan - 1, 0), jnp.minimum(tan + 1, tans - 1)))
    end, middle = pos == 0, pos == half - 1

    barrier = pltpu.get_barrier_semaphore()
    greeted = mates + crew + [inward]
    for who in greeted:
        pl.semaphore_signal(barrier, inc=1, device_id=who, device_id_type=MESH)

    @pl.when(jnp.logical_not(end))
    def _():
        pl.semaphore_signal(barrier, inc=1, device_id=outward, device_id_type=MESH)

    load_part = pltpu.make_async_copy(part.at[core], x, s_part)
    load_part.start()
    load_share = pltpu.make_async_copy(share_in, share, s_share)
    load_share.start()

    @pl.when(end)
    def _():
        pl.semaphore_wait(barrier, len(greeted))

    @pl.when(jnp.logical_not(end))
    def _():
        pl.semaphore_wait(barrier, len(greeted) + 1)

    def copy(src, dst, s, r, who):
        return pltpu.make_async_remote_copy(
            src_ref=src, dst_ref=dst, send_sem=s, recv_sem=r, device_id=who, device_id_type=MESH
        )

    firsts = []
    for d in list(range(1, teams)) + [0]:
        to_team = lax.rem(team + d, teams)
        c = copy(part.at[1 - core, to_team], r1.at[to_team], s_core.at[d], r_core.at[d], mates[0])
        c.start()
        firsts.append((d, to_team, c))

    def mine(k):
        return a2 if k == chunks else share.at[pl.ds(k * size, size)]

    def inner_of(k):
        return inner_w if k == chunks else inner.at[k]

    def outer_of(k):
        return outer_w if k == chunks else outer.at[k]

    def fin_of(k):
        return fin_w if k == chunks else fin.at[k]

    def in_copy(src, k):
        return copy(src, inner_of(k), s_in.at[k], r_in.at[k], inward)

    def cross_copy(src, k):
        return copy(src, fin_of(k), s_in.at[k], r_fin.at[k], inward)

    def out_copy(k):
        return copy(fin_of(k), fin_of(k), s_out.at[k], r_fin.at[k], outward)

    def send_in(src, k):
        @pl.when(middle)
        def _():
            cross_copy(src, k).start()

        @pl.when(jnp.logical_not(middle))
        def _():
            in_copy(src, k).start()

    def begin(k):
        @pl.when(end)
        def _():
            send_in(a2 if k == chunks else share_in.at[pl.ds(k * size, size)], k)

    def relay(k):
        @pl.when(jnp.logical_not(end))
        def _():
            in_copy(mine(k), k).wait_recv()
            outer_of(k)[...] = mine(k)[...] + inner_of(k)[...]
            send_in(outer_of(k), k)

    def finish(k):
        cross_copy(mine(k), k).wait_recv()
        f = fin_of(k)

        @pl.when(jnp.logical_and(middle, end))
        def _():
            f[...] = mine(k)[...] + f[...]

        @pl.when(jnp.logical_and(middle, jnp.logical_not(end)))
        def _():
            f[...] = outer_of(k)[...] + f[...]

        @pl.when(jnp.logical_not(end))
        def _():
            out_copy(k).start()

    for k in range(chunks):
        begin(k)

    load_part.wait()
    load_share.wait()
    seconds = []
    for d, to_team, got in firsts:
        got.wait()
        a1[to_team] = x[to_team] + r1[to_team]
        if d > 0:
            c = copy(a1.at[to_team], r2.at[d - 1], s_chip.at[d - 1], r_chip.at[d - 1], crew[d - 1])
            c.start()
            seconds.append(c)

    ahead = chunks - 3 if chunks > 3 else chunks
    for k in range(ahead):
        relay(k)

    for c in seconds:
        c.wait()
    total = a1[team]
    for d in range(teams - 1):
        total = total + r2[d]
    a2[...] = total
    begin(chunks)
    order = list(range(ahead, chunks))
    for k in order[:1] + [chunks] + order[1:]:
        relay(k)

    def deliver(k):
        finish(k)
        pre_out[pl.ds(k * size, size), :] = fin[k]

    for k in range(ahead):
        deliver(k)
    finish(chunks)
    y[core, team] = fin_w[...]
    lasts = []

    def pass_on(d, from_team):
        c = copy(y.at[core, from_team], y.at[core, from_team], s_last.at[d], r_last.at[d], mates[0])
        c.start()
        lasts.append(c)

    fourths = []
    for d in range(1, teams):
        c = copy(y.at[core, team], y.at[core, team], s_back.at[d - 1], r_back.at[d - 1], crew[d - 1])
        c.start()
        fourths.append(c)
    pass_on(0, team)
    for k in order:
        deliver(k)
    for d in range(1, teams):
        fourths[d - 1].wait()
        pass_on(d, lax.rem(team - d + teams, teams))
    for c in lasts:
        c.wait()
    y_out[...] = y[...]

    for k in range(chunks + 1):
        cross_copy(mine(k), k).wait_send()

        @pl.when(jnp.logical_not(end))
        def _():
            out_copy(k).wait_send()


def finish_kernel(walks, pre, y, cot_primal, weight, grad_primal, grad_w, grad_b):
    piece = grad_w.shape[0] // walks
    grad_primal[...] = cot_primal[...] + wide_mm(pre[...], weight[...], TRANS_B)
    for c in range(2):
        for k in range(walks // 2):
            at = (k * 2 + c) * piece
            grad_w[at : at + piece, :] = y[c, k, 0:piece, :]
    grad_b[...] = y[0, 0, piece : piece + 1, :]


def per_device(walks, tans, primal, laplace, tangent, cot_primal, cot_tangent, cot_laplace, weight, bias):
    walkers, electrons, width = primal.shape
    channels = tangent.shape[0]
    rows = walkers * electrons
    flat = [z.reshape(rows, width) for z in (primal, laplace, cot_primal, cot_laplace)]
    tan_flat = tangent.reshape(channels, rows, width)
    cot_flat = cot_tangent.reshape(channels, rows, width)
    bias_row = bias.reshape(1, width)
    block = electrons
    group = next(g for g in (8, 6, 4, 3, 2, 1) if channels % g == 0)
    span = next(g for g in (2, 3, 1) if channels // group % g == 0)
    row_spec = pl.BlockSpec((block, width), lambda i: (i, 0))
    tan_spec = pl.BlockSpec((channels, block, width), lambda i: (0, i, 0))

    def whole(shape):
        return pl.BlockSpec(shape, lambda i: (0,) * len(shape))

    teams = walks // 2
    piece = width // walks + 8
    grad_lap, grad_tan, share, part = pl.pallas_call(
        functools.partial(local_kernel, group, span, tans),
        grid=(rows // block,),
        in_specs=[row_spec, row_spec, tan_spec, row_spec, tan_spec, row_spec, whole((width, width)), whole((1, width))],
        out_specs=[row_spec, tan_spec, row_spec, whole((2, teams, piece, width))],
        out_shape=[
            jax.ShapeDtypeStruct((rows, width), F32),
            jax.ShapeDtypeStruct(tan_flat.shape, BF16),
            jax.ShapeDtypeStruct((rows, width), F32),
            jax.ShapeDtypeStruct((2, teams, piece, width), F32),
        ],
        scratch_shapes=[pltpu.VMEM((width, width), F32), pltpu.VMEM((8, width), F32)]
        + [pltpu.VMEM((channels, block, width), F32), pltpu.VMEM((channels, block, width), BF16)]
        + [pltpu.VMEM((block, width), F32)] * 4,
        compiler_params=pltpu.CompilerParams(vmem_limit_bytes=VMEM_ALL),
        name="local",
    )(flat[0], flat[1], tan_flat, flat[2], cot_flat, flat[3], weight, bias_row)

    chunks = walkers * 2
    size = rows // chunks
    vmem = pl.BlockSpec(memory_space=pltpu.VMEM)
    dma = pltpu.SemaphoreType.DMA
    crew = max(teams - 1, 1)
    pre_sum, y = pl.pallas_call(
        functools.partial(sum_kernel, walks, tans, chunks),
        in_specs=[pl.BlockSpec(memory_space=pl.ANY)] * 2,
        out_specs=[vmem] * 2,
        out_shape=[
            jax.ShapeDtypeStruct((rows, width), F32),
            jax.ShapeDtypeStruct((2, teams, piece, width), F32),
        ],
        scratch_shapes=[
            pltpu.VMEM((rows, width), F32),
            pltpu.VMEM((teams, piece, width), F32),
            pltpu.VMEM((teams, piece, width), F32),
            pltpu.VMEM((teams, piece, width), F32),
            pltpu.VMEM((crew, piece, width), F32),
            pltpu.VMEM((piece, width), F32),
            pltpu.VMEM((chunks, size, width), F32),
            pltpu.VMEM((chunks, size, width), F32),
            pltpu.VMEM((chunks, size, width), F32),
            pltpu.VMEM((piece, width), F32),
            pltpu.VMEM((piece, width), F32),
            pltpu.VMEM((piece, width), F32),
            pltpu.VMEM((2, teams, piece, width), F32),
            dma((teams,)), dma((teams,)),
            dma((crew,)), dma((crew,)),
            dma((crew,)), dma((crew,)),
            dma((teams,)), dma((teams,)),
            dma((chunks + 1,)), dma((chunks + 1,)), dma((chunks + 1,)), dma((chunks + 1,)),
            dma, dma,
        ],
        compiler_params=pltpu.CompilerParams(collective_id=0, has_side_effects=True, vmem_limit_bytes=VMEM_ALL),
        name="sums",
    )(share, part)
    grad_primal, grad_w, grad_b = pl.pallas_call(
        functools.partial(finish_kernel, walks),
        in_specs=[vmem] * 4,
        out_specs=[vmem] * 3,
        out_shape=[
            jax.ShapeDtypeStruct((rows, width), F32),
            jax.ShapeDtypeStruct((width, width), F32),
            jax.ShapeDtypeStruct((1, width), F32),
        ],
        compiler_params=pltpu.CompilerParams(vmem_limit_bytes=VMEM_ALL),
        name="finish",
    )(pre_sum, y, flat[2], weight)
    return (
        grad_primal.reshape(primal.shape),
        grad_lap.reshape(primal.shape),
        grad_tan.reshape(tangent.shape),
        grad_w,
        grad_b.reshape(bias.shape),
    )


def solution(mesh):
    return jax.shard_map(
        functools.partial(per_device, mesh.shape["walk"], mesh.shape["tan"]),
        mesh=mesh,
        in_specs=(
            P("walk", None, None),
            P("walk", None, None),
            P("tan", "walk", None, None),
            P("walk", None, None),
            P("tan", "walk", None, None),
            P("walk", None, None),
            P(),
            P(),
        ),
        out_specs=(
            P("walk", None, None),
            P("walk", None, None),
            P("tan", "walk", None, None),
            P(),
            P(),
        ),
        check_vma=False,
    )
```

```python
import functools

import jax
import jax.numpy as jnp
from jax import lax
from jax.experimental import pallas as pl
from jax.experimental.pallas import tpu as pltpu
from jax.sharding import PartitionSpec as P

F32 = jnp.float32
BF16 = jnp.bfloat16
MESH = pl.DeviceIdType.MESH
VMEM_ALL = 67_043_328
TRANS_B = (((1,), (1,)), ((), ()))
TRANS_A = (((0,), (0,)), ((), ()))
PLAIN = (((1,), (0,)), ((), ()))


def mm(a, b, dims=PLAIN):
    return lax.dot_general(a, b, dims, preferred_element_type=F32)


def halves(x):
    top = x.astype(BF16)
    return top, (x - top.astype(F32)).astype(BF16)


def wide_mm(x, w, dims):
    top, low = halves(x)
    return mm(top, w, dims) + mm(low, w, dims)


def wide_outer(x, y):
    xt, xl = halves(x)
    yt, yl = halves(y)
    return mm(xt, yt, TRANS_A) + mm(xt, yl, TRANS_A) + mm(xl, yt, TRANS_A)


def local_kernel(
    group, span, shares, primal, laplace, tangent, cot_primal, cot_tangent, cot_laplace, weight, bias,
    grad_lap, grad_tan, share, part, grad_w, grad_b, moved, moved_back, slope, gain, squares, crossed,
):
    channels, rows, width = tangent.shape
    w = weight[...]
    pre = wide_mm(primal[...], w, PLAIN) + bias[...]
    t = jnp.tanh(pre)
    s1 = 1.0 - t * t
    s2 = -2.0 * t * s1
    s3 = (6.0 * t * t - 2.0) * s1
    lz = wide_mm(laplace[...], w, PLAIN)
    cl = cot_laplace[...]
    g_lz = cl * s1
    grad_lap[...] = cl + wide_mm(g_lz, w, TRANS_B)
    slope[...] = s1
    gain[...] = 2.0 * s2 * cl
    tile = 16
    flat_rows = group * rows
    count = channels // group

    def forward(j):
        at = pl.ds(j * group, group)
        moved[at] = mm(tangent[at].reshape(flat_rows, width), w).reshape(group, rows, width)

    def middle(j):
        for k in range(0, rows, tile):
            row = pl.ds(k, tile)
            s, a = slope[row, :], gain[row, :]
            if j == 0:
                q = jnp.zeros((tile, width), F32)
                r = jnp.zeros((tile, width), F32)
            else:
                q, r = squares[row, :], crossed[row, :]
            for c in range(j * group, (j + 1) * group):
                dz = moved[c, row, :]
                cot = cot_tangent[c, row, :].astype(F32)
                q = q + dz * dz
                r = r + cot * dz
                moved_back[c, row, :] = (s * cot + a * dz).astype(BF16)
            squares[row, :], crossed[row, :] = q, r

    def backward(j):
        at = pl.ds(j * group, group)
        g = moved_back[at].reshape(flat_rows, width)
        back = mm(g, w, TRANS_B).reshape(group, rows, width)
        grad_tan[at] = (cot_tangent[at].astype(F32) + back).astype(BF16)

    @pl.when(pl.program_id(0) == 0)
    def _():
        grad_w[...] = jnp.zeros_like(grad_w)
        grad_b[...] = jnp.zeros_like(grad_b)

    forward(0)
    for j in range(count):
        if j + 1 < count:
            forward(j + 1)
        middle(j)
        if j > 0:
            backward(j - 1)
        if (j + 1) % span == 0:
            at = pl.ds((j + 1 - span) * group, span * group)
            deep = span * flat_rows
            grad_w[...] += mm(tangent[at].reshape(deep, width), moved_back[at].reshape(deep, width), TRANS_A)
    backward(count - 1)
    v = (cl * s3 * squares[...] + s2 * crossed[...]) + (cot_primal[...] * s1 + cl * (s2 * lz)) * (1.0 / shares)
    share[...] = v
    grad_w[...] += wide_outer(primal[...], v) + wide_outer(laplace[...], g_lz * (1.0 / shares))
    grad_b[...] += jnp.broadcast_to(jnp.sum(v, 0, keepdims=True), grad_b.shape)

    @pl.when(pl.program_id(0) == pl.num_programs(0) - 1)
    def _():
        piece = part.shape[2] - 8
        for c in range(2):
            for k in range(part.shape[1]):
                at = (k * 2 + c) * piece
                part[c, k, 0:piece, :] = grad_w[at : at + piece, :]
                part[c, k, piece:, :] = grad_b[...]


def sum_kernel(
    walks, tans, chunks, share_in, part,
    pre_out, y_out,
    share, x, r1, a1, r2, a2, inner, outer, fin, inner_w, outer_w, fin_w, y,
    s_core, r_core, s_chip, r_chip, s_back, r_back, s_last, r_last,
    s_in, r_in, r_fin, s_out, s_share, s_part, s_pre,
):
    teams = walks // 2
    walk, tan = lax.axis_index("walk"), lax.axis_index("tan")
    core, team = lax.rem(walk, 2), walk // 2
    mate = team * 2 + (1 - core)
    size = share.shape[0] // chunks

    def to(w, t):
        return (w, t)

    mates = [to(mate, tan)]
    crew = [to(lax.rem(team + d, teams) * 2 + core, tan) for d in range(1, teams)]
    half = tans // 2
    left = tan < half
    pos = jnp.where(left, tan, tans - 1 - tan)
    inward = to(walk, jnp.where(left, tan + 1, tan - 1))
    outward = to(walk, jnp.where(left, jnp.maximum(tan - 1, 0), jnp.minimum(tan + 1, tans - 1)))
    end, middle = pos == 0, pos == half - 1

    barrier = pltpu.get_barrier_semaphore()
    greeted = mates + crew + [inward]
    for who in greeted:
        pl.semaphore_signal(barrier, inc=1, device_id=who, device_id_type=MESH)

    @pl.when(jnp.logical_not(end))
    def _():
        pl.semaphore_signal(barrier, inc=1, device_id=outward, device_id_type=MESH)

    load_part = pltpu.make_async_copy(part.at[core], x, s_part)
    load_part.start()
    load_share = pltpu.make_async_copy(share_in, share, s_share)
    load_share.start()

    @pl.when(end)
    def _():
        pl.semaphore_wait(barrier, len(greeted))

    @pl.when(jnp.logical_not(end))
    def _():
        pl.semaphore_wait(barrier, len(greeted) + 1)

    def copy(src, dst, s, r, who):
        return pltpu.make_async_remote_copy(
            src_ref=src, dst_ref=dst, send_sem=s, recv_sem=r, device_id=who, device_id_type=MESH
        )

    firsts = []
    for d in list(range(1, teams)) + [0]:
        to_team = lax.rem(team + d, teams)
        c = copy(part.at[1 - core, to_team], r1.at[to_team], s_core.at[d], r_core.at[d], mates[0])
        c.start()
        firsts.append((d, to_team, c))

    def mine(k):
        return a2 if k == chunks else share.at[pl.ds(k * size, size)]

    def inner_of(k):
        return inner_w if k == chunks else inner.at[k]

    def outer_of(k):
        return outer_w if k == chunks else outer.at[k]

    def fin_of(k):
        return fin_w if k == chunks else fin.at[k]

    def in_copy(src, k):
        return copy(src, inner_of(k), s_in.at[k], r_in.at[k], inward)

    def cross_copy(src, k):
        return copy(src, fin_of(k), s_in.at[k], r_fin.at[k], inward)

    def out_copy(k):
        return copy(fin_of(k), fin_of(k), s_out.at[k], r_fin.at[k], outward)

    def send_in(src, k):
        @pl.when(middle)
        def _():
            cross_copy(src, k).start()

        @pl.when(jnp.logical_not(middle))
        def _():
            in_copy(src, k).start()

    def begin(k):
        @pl.when(end)
        def _():
            send_in(a2 if k == chunks else share_in.at[pl.ds(k * size, size)], k)

    def relay(k):
        @pl.when(jnp.logical_not(end))
        def _():
            in_copy(mine(k), k).wait_recv()
            outer_of(k)[...] = mine(k)[...] + inner_of(k)[...]
            send_in(outer_of(k), k)

    def finish(k):
        cross_copy(mine(k), k).wait_recv()
        f = fin_of(k)

        @pl.when(jnp.logical_and(middle, end))
        def _():
            f[...] = mine(k)[...] + f[...]

        @pl.when(jnp.logical_and(middle, jnp.logical_not(end)))
        def _():
            f[...] = outer_of(k)[...] + f[...]

        @pl.when(jnp.logical_not(end))
        def _():
            out_copy(k).start()

    for k in range(chunks):
        begin(k)

    load_part.wait()
    load_share.wait()
    seconds = []
    for d, to_team, got in firsts:
        got.wait()
        a1[to_team] = x[to_team] + r1[to_team]
        if d > 0:
            c = copy(a1.at[to_team], r2.at[d - 1], s_chip.at[d - 1], r_chip.at[d - 1], crew[d - 1])
            c.start()
            seconds.append(c)

    ahead = chunks - 3 if chunks > 3 else chunks
    for k in range(ahead):
        relay(k)

    for c in seconds:
        c.wait()
    total = a1[team]
    for d in range(teams - 1):
        total = total + r2[d]
    a2[...] = total
    begin(chunks)
    order = list(range(ahead, chunks))
    for k in order[:1] + [chunks] + order[1:]:
        relay(k)

    def write(k):
        return pltpu.make_async_copy(fin.at[k], pre_out.at[pl.ds(k * size, size)], s_pre.at[k])

    def deliver(k):
        finish(k)
        write(k).start()

    for k in range(ahead):
        deliver(k)
    finish(chunks)
    y[core, team] = fin_w[...]
    lasts = []

    def pass_on(d, from_team):
        c = copy(y.at[core, from_team], y.at[core, from_team], s_last.at[d], r_last.at[d], mates[0])
        c.start()
        lasts.append(c)

    fourths = []
    for d in range(1, teams):
        c = copy(y.at[core, team], y.at[core, team], s_back.at[d - 1], r_back.at[d - 1], crew[d - 1])
        c.start()
        fourths.append(c)
    pass_on(0, team)
    for k in order:
        deliver(k)
    for d in range(1, teams):
        fourths[d - 1].wait()
        pass_on(d, lax.rem(team - d + teams, teams))
    for c in lasts:
        c.wait()
    write_y = pltpu.make_async_copy(y, y_out, s_part)
    write_y.start()
    for k in range(chunks):
        write(k).wait()
    write_y.wait()

    for k in range(chunks + 1):
        cross_copy(mine(k), k).wait_send()

        @pl.when(jnp.logical_not(end))
        def _():
            out_copy(k).wait_send()


def finish_kernel(walks, pre, y, cot_primal, weight, grad_primal, grad_w, grad_b):
    piece = grad_w.shape[0] // walks
    grad_primal[...] = cot_primal[...] + wide_mm(pre[...], weight[...], TRANS_B)
    for c in range(2):
        for k in range(walks // 2):
            at = (k * 2 + c) * piece
            grad_w[at : at + piece, :] = y[c, k, 0:piece, :]
    grad_b[...] = y[0, 0, piece : piece + 1, :]


def per_device(walks, tans, primal, laplace, tangent, cot_primal, cot_tangent, cot_laplace, weight, bias):
    walkers, electrons, width = primal.shape
    channels = tangent.shape[0]
    rows = walkers * electrons
    flat = [z.reshape(rows, width) for z in (primal, laplace, cot_primal, cot_laplace)]
    tan_flat = tangent.reshape(channels, rows, width)
    cot_flat = cot_tangent.reshape(channels, rows, width)
    bias_row = bias.reshape(1, width)
    block = electrons
    group = next(g for g in (8, 6, 4, 3, 2, 1) if channels % g == 0)
    span = next(g for g in (2, 3, 1) if channels // group % g == 0)
    row_spec = pl.BlockSpec((block, width), lambda i: (i, 0))
    tan_spec = pl.BlockSpec((channels, block, width), lambda i: (0, i, 0))

    def whole(shape):
        return pl.BlockSpec(shape, lambda i: (0,) * len(shape))

    teams = walks // 2
    piece = width // walks + 8
    grad_lap, grad_tan, share, part = pl.pallas_call(
        functools.partial(local_kernel, group, span, tans),
        grid=(rows // block,),
        in_specs=[row_spec, row_spec, tan_spec, row_spec, tan_spec, row_spec, whole((width, width)), whole((1, width))],
        out_specs=[row_spec, tan_spec, row_spec, whole((2, teams, piece, width))],
        out_shape=[
            jax.ShapeDtypeStruct((rows, width), F32),
            jax.ShapeDtypeStruct(tan_flat.shape, BF16),
            jax.ShapeDtypeStruct((rows, width), F32),
            jax.ShapeDtypeStruct((2, teams, piece, width), F32),
        ],
        scratch_shapes=[pltpu.VMEM((width, width), F32), pltpu.VMEM((8, width), F32)]
        + [pltpu.VMEM((channels, block, width), F32), pltpu.VMEM((channels, block, width), BF16)]
        + [pltpu.VMEM((block, width), F32)] * 4,
        compiler_params=pltpu.CompilerParams(vmem_limit_bytes=VMEM_ALL),
        name="local",
    )(flat[0], flat[1], tan_flat, flat[2], cot_flat, flat[3], weight, bias_row)

    chunks = walkers * 2
    size = rows // chunks
    vmem = pl.BlockSpec(memory_space=pltpu.VMEM)
    dma = pltpu.SemaphoreType.DMA
    crew = max(teams - 1, 1)
    pre_sum, y = pl.pallas_call(
        functools.partial(sum_kernel, walks, tans, chunks),
        in_specs=[pl.BlockSpec(memory_space=pl.ANY)] * 2,
        out_specs=[pl.BlockSpec(memory_space=pl.ANY)] * 2,
        out_shape=[
            jax.ShapeDtypeStruct((rows, width), F32),
            jax.ShapeDtypeStruct((2, teams, piece, width), F32),
        ],
        scratch_shapes=[
            pltpu.VMEM((rows, width), F32),
            pltpu.VMEM((teams, piece, width), F32),
            pltpu.VMEM((teams, piece, width), F32),
            pltpu.VMEM((teams, piece, width), F32),
            pltpu.VMEM((crew, piece, width), F32),
            pltpu.VMEM((piece, width), F32),
            pltpu.VMEM((chunks, size, width), F32),
            pltpu.VMEM((chunks, size, width), F32),
            pltpu.VMEM((chunks, size, width), F32),
            pltpu.VMEM((piece, width), F32),
            pltpu.VMEM((piece, width), F32),
            pltpu.VMEM((piece, width), F32),
            pltpu.VMEM((2, teams, piece, width), F32),
            dma((teams,)), dma((teams,)),
            dma((crew,)), dma((crew,)),
            dma((crew,)), dma((crew,)),
            dma((teams,)), dma((teams,)),
            dma((chunks + 1,)), dma((chunks + 1,)), dma((chunks + 1,)), dma((chunks + 1,)),
            dma, dma, dma((chunks,)),
        ],
        compiler_params=pltpu.CompilerParams(collective_id=0, has_side_effects=True, vmem_limit_bytes=VMEM_ALL),
        name="sums",
    )(share, part)
    grad_primal, grad_w, grad_b = pl.pallas_call(
        functools.partial(finish_kernel, walks),
        in_specs=[vmem] * 4,
        out_specs=[vmem] * 3,
        out_shape=[
            jax.ShapeDtypeStruct((rows, width), F32),
            jax.ShapeDtypeStruct((width, width), F32),
            jax.ShapeDtypeStruct((1, width), F32),
        ],
        compiler_params=pltpu.CompilerParams(vmem_limit_bytes=VMEM_ALL),
        name="finish",
    )(pre_sum, y, flat[2], weight)
    return (
        grad_primal.reshape(primal.shape),
        grad_lap.reshape(primal.shape),
        grad_tan.reshape(tangent.shape),
        grad_w,
        grad_b.reshape(bias.shape),
    )


def solution(mesh):
    return jax.shard_map(
        functools.partial(per_device, mesh.shape["walk"], mesh.shape["tan"]),
        mesh=mesh,
        in_specs=(
            P("walk", None, None),
            P("walk", None, None),
            P("tan", "walk", None, None),
            P("walk", None, None),
            P("tan", "walk", None, None),
            P("walk", None, None),
            P(),
            P(),
        ),
        out_specs=(
            P("walk", None, None),
            P("walk", None, None),
            P("tan", "walk", None, None),
            P(),
            P(),
        ),
        check_vma=False,
    )
```
